128 devices in a mesh: prompt: 8 (over y_hi, z), slot: 16 (over x, y_lo, core).
Axes of the slice: x: 4, y: 4 (y_hi: 2, y_lo: 2; y = y_hi * 2 + y_lo), z: 4, core: 2. Of those that a mesh axis runs over, the one named last changes fastest.
Arguments:
- patch_kv: bfloat16 [8, 256, 128, 2048], P('prompt', 'slot'), may hold values from -6 to 6
- routes: int32 [8, 256], P('prompt', 'slot'), may hold values from -1 to 15, as said below
- prefix_kv: bfloat16 [8, 512, 2048], P('prompt', None, 'slot'), may hold values from -4 to 4
- prefix_len: int32 [8], P('prompt'), may hold values from 1 to 512, 3072 in all
- queries: bfloat16 [8, 16, 256, 8192], P('prompt', 'slot'), may hold values from -160 to 160
- suffix_kv: bfloat16 [8, 16, 256, 2048], P('prompt', 'slot'), may hold values from -6 to 6
- score_head: float32 [8192], replicated, may hold values from -0.0625 to 0.0625
Outputs:
- context: bfloat16 [8, 16, 256, 8192], P('prompt', 'slot')
- advantage: float32 [8, 16], P('prompt', 'slot')
The draws below stay inside these ranges and needn't reach their ends.
Inputs may be any that keep to these rules, and one draw needn't show every extreme that they name: `routes`: in the list of one generating device each judge index appears at most once, and in one prompt's lists each judge index appears exactly 8 times; -1 marks an empty slot.
All inputs are finite; a program needn't handle non-finite values. No bound on the sum of `prefix_len` on one device may be relied on, other than what follows from the above.
Results may differ from the reference program's by a relative error of at most 0.005.
Values may be sent and summed in bfloat16 or wider, within the bound.
A program may use at most 128 MiB of HBM per device.

```python
import math
import jax
import jax.numpy as jnp
import numpy as np
from jax import lax

HEADS = 64
KVH = 8
HD = 128
PREFIX = 512
SUF = 256
TILE = 128
PROMPTS = 8
IMG_TILES = 8
IMG = 1024
KVW = 2048
QW = 8192
N_SLOT = 16


def prefix_values(key):
    values = jax.random.normal(jax.random.fold_in(key, 11), (PROMPTS, PREFIX, KVW), jnp.float32)
    return jnp.clip(values, -4.0, 4.0)


def draw_prefix_kv(key, part):
    return prefix_values(key).astype(jnp.bfloat16)


def draw_queries(key, part):
    values = jax.random.normal(jax.random.fold_in(key, 12), (PROMPTS, N_SLOT, SUF, HEADS * HD), jnp.float32)
    values = jnp.clip(values, -6.0, 6.0)
    return values.astype(jnp.bfloat16)


def draw_routes(key, part):

    def one_prompt(prompt_key):
        judge_keys = jax.random.split(jax.random.fold_in(prompt_key, 1), N_SLOT)
        senders = jax.vmap(lambda k: jax.random.permutation(k, N_SLOT))(judge_keys)
        ranking = jnp.argsort(senders, axis=1)
        chosen = ranking < N_SLOT // 2
        source_keys = jax.random.split(jax.random.fold_in(prompt_key, 2), N_SLOT)
        layout = jax.vmap(lambda k: jax.random.permutation(k, N_SLOT))(source_keys)
        sources = jnp.arange(N_SLOT)[:, None]
        taken = chosen[layout, sources]
        return jnp.where(taken, layout, -1).reshape(N_SLOT * N_SLOT)
    prompt_keys = jax.random.split(jax.random.fold_in(key, 13), PROMPTS)
    return jax.vmap(one_prompt)(prompt_keys).astype(jnp.int32)


def block_levels(own_key, dims, cuts, low, largest):
    level, own = 1.0, jax.random.fold_in(own_key, 6)
    for axis_at, blocks in cuts:
        draws = jnp.exp(jax.random.uniform(jax.random.fold_in(own, axis_at), (blocks,), jnp.float32, low / len(cuts), largest / len(cuts)))
        level = level * jnp.repeat(draws, dims[axis_at] // blocks).reshape([-1 if axis == axis_at else 1 for axis in range(len(dims))])
    return level


def length_profile(number_of, total, reach, slope):
    loads = [(1 << 20) // math.isqrt(standing ** slope) + 1 for standing in range(2, number_of + 1)]
    rest, counts = total - reach - (number_of - 1), [1] * (number_of - 1)
    while rest > 0:
        movable = [i for i in range(number_of - 1) if counts[i] < reach]
        mass, budget = sum([loads[i] for i in movable]), rest
        for i in movable:
            addition = min(reach - counts[i], max(1, budget * loads[i] // mass), rest)
            counts[i] = counts[i] + addition
            rest = rest - addition
    return np.array([reach] + counts)


def ragged(stream_key, count, total, bound, lean):
    if count == 2:
        one = jax.random.randint(stream_key, (), max(1, total - bound), min(bound, total - 1) + 1)
        return jnp.stack([one, total - one])
    lengths = jnp.asarray(length_profile(count, total, bound, lean), jnp.int32)
    couples = (count - 1) // 2
    source_of, taker = lengths[1:1 + 2 * couples:2], lengths[2:2 + 2 * couples:2]
    margin = jnp.minimum(source_of - 1, bound - taker)
    shifted = jax.random.randint(jax.random.fold_in(stream_key, 1), (couples,), 0, 1 << 20) % (margin + 1)
    lengths = lengths.at[1:1 + 2 * couples:2].set(source_of - shifted).at[2:2 + 2 * couples:2].set(taker + shifted)
    return lengths[jax.random.permutation(jax.random.fold_in(stream_key, 2), count)]


def centred(key, shape, scale, limit, cuts=(), kind=jnp.bfloat16):
    level = block_levels(key, shape, cuts, -0.22, 0.18) if cuts else 1.0
    values = jax.random.normal(key, shape, jnp.float32) * scale * level
    return jnp.minimum(jnp.maximum(values, -limit), limit).astype(kind)


def setup_inputs(seed: int = 0) -> dict:
    splits = jax.random.split(jax.random.key(seed), 8)
    patch_kv = centred(splits[0], (PROMPTS, N_SLOT * N_SLOT, TILE, KVW), 1.0, 6.0, ((0, 8), (1, 16)))
    routes = draw_routes(jax.random.fold_in(splits[7], 71), 0)
    prefix_kv = draw_prefix_kv(jax.random.fold_in(splits[7], 71), 0)
    prefix_len = ragged(splits[3], PROMPTS, PROMPTS * PREFIX * 3 // 4, PREFIX, 1).astype(jnp.int32)
    queries = draw_queries(jax.random.fold_in(splits[7], 71), 0)
    suffix_kv = centred(splits[5], (PROMPTS, N_SLOT, SUF, KVW), 1.0, 6.0, ((0, 8), (1, 16)))
    score_head = centred(splits[6], (QW,), QW ** -0.5, 0.0625, (), jnp.float32)
    return {"patch_kv": patch_kv, "routes": routes, "prefix_kv": prefix_kv, "prefix_len": prefix_len, "queries": queries, "suffix_kv": suffix_kv, "score_head": score_head}


def head_attention(query_rows, key_rows, value_rows, allowed):
    factor = 1.0 / math.sqrt(HD)
    scores = jnp.einsum('sgd,kd->gsk', query_rows.astype(jnp.float32), key_rows.astype(jnp.float32)) * factor
    scores = jnp.where(allowed[None, :, :], scores, -1e+30)
    peak = lax.optimization_barrier(jnp.max(scores, axis=-1, keepdims=True))
    weights = jnp.exp(scores - peak)
    totals = lax.optimization_barrier(jnp.sum(weights, axis=-1))
    rounded = weights.astype(jnp.bfloat16)
    mixed = jnp.einsum('gsk,kd->sgd', rounded.astype(jnp.float32), value_rows.astype(jnp.float32))
    return mixed / jnp.transpose(totals)[:, :, None]

def reference(patch_kv, routes, prefix_kv, prefix_len, queries, suffix_kv, score_head):
    groups = HEADS // KVH

    def one_image(pair):
        prompt = pair[0]
        judge = pair[1]
        found = jnp.nonzero(routes[prompt] == judge, size=IMG_TILES)[0].astype(jnp.int32)
        image_rows = patch_kv[prompt][found].reshape(IMG, KVW)
        rows_all = jnp.concatenate([prefix_kv[prompt], image_rows, suffix_kv[prompt, judge]], axis=0)
        columns = jnp.arange(PREFIX + IMG + SUF, dtype=jnp.int32)[None, :]
        positions = jnp.arange(SUF, dtype=jnp.int32)[:, None]
        allowed = jnp.where(columns < PREFIX, columns < prefix_len[prompt], jnp.where(columns < PREFIX + IMG, True, columns - PREFIX - IMG <= positions))
        own_queries = queries[prompt, judge]
        pieces = []
        for group in range(KVH):
            query_rows = own_queries[:, group * groups * HD:(group + 1) * groups * HD].reshape(SUF, groups, HD)
            key_rows = rows_all[:, group * HD:(group + 1) * HD]
            value_rows = rows_all[:, (KVH + group) * HD:(KVH + group + 1) * HD]
            pieces.append(head_attention(query_rows, key_rows, value_rows, allowed).reshape(SUF, groups * HD))
        return jnp.concatenate(pieces, axis=1).astype(jnp.bfloat16)
    prompt_ids = jnp.repeat(jnp.arange(PROMPTS, dtype=jnp.int32), N_SLOT)
    judge_ids = jnp.tile(jnp.arange(N_SLOT, dtype=jnp.int32), PROMPTS)
    context = lax.map(one_image, jnp.stack([prompt_ids, judge_ids], axis=1))
    context = context.reshape(PROMPTS, N_SLOT, SUF, HEADS * HD)
    last_rows = context[:, :, SUF - 1, :].astype(jnp.float32).reshape(PROMPTS * N_SLOT, HEADS * HD)
    score = jnp.dot(last_rows, score_head, precision=lax.Precision.HIGHEST, preferred_element_type=jnp.float32).reshape(PROMPTS, N_SLOT)
    centre = lax.optimization_barrier(jnp.sum(score, axis=1, keepdims=True)) / N_SLOT
    deviation = score - centre
    spread = jnp.sum(deviation * deviation) / (PROMPTS * N_SLOT)
    advantage = deviation / jnp.sqrt(spread + 1e-06)
    return (context, advantage)
```

```python
import math

import jax
import jax.numpy as jnp
from jax import lax
from jax.experimental import pallas as pl
from jax.experimental.pallas import tpu as pltpu
from jax.sharding import PartitionSpec as P

HEADS = 64
KVH = 8
HD = 128
GROUPS = HEADS // KVH
MESH = pl.DeviceIdType.MESH
OFFSETS = (
    (1, 0, 0), (3, 0, 0), (0, 1, 0), (2, 0, 0), (1, 1, 0),
    (3, 1, 0), (0, 1, 1), (2, 1, 0), (1, 0, 1), (3, 0, 1),
    (2, 0, 1), (1, 1, 1), (3, 1, 1), (2, 1, 1), (0, 0, 1),
)
NEG = -1e30


def pack_kernel(routes_ref, patch_ref, out_ref, live_ref):
    for g in range(KVH):
        out_ref[g, 0, :, :HD] = patch_ref[0, :, g * HD:(g + 1) * HD]
        out_ref[g, 0, :, HD:] = patch_ref[0, :, (KVH + g) * HD:(KVH + g + 1) * HD]

    @pl.when(pl.program_id(0) == 0)
    def _():
        lane = lax.broadcasted_iota(jnp.int32, live_ref.shape, 1)
        live = jnp.zeros(live_ref.shape, jnp.int32)
        for k in range(routes_ref.shape[1]):
            live = live + jnp.where(lane == routes_ref[0, k], 1, 0)
        live_ref[...] = live


def pack(routes, patch):
    slots, rows, width = patch.shape

    def source(d, routes_ref):
        slot = jnp.int32(0)
        for k in range(slots):
            slot = jnp.where(routes_ref[0, k] == d, jnp.int32(k), slot)
        return (slot, 0, 0)

    return pl.pallas_call(
        pack_kernel,
        grid_spec=pltpu.PrefetchScalarGridSpec(
            num_scalar_prefetch=1,
            grid=(slots,),
            in_specs=[pl.BlockSpec((1, rows, width), source)],
            out_specs=[
                pl.BlockSpec((KVH, 1, rows, 2 * HD), lambda d, r: (0, d, 0, 0)),
                pl.BlockSpec((8, 128), lambda d, r: (0, 0)),
            ],
        ),
        out_shape=[
            jax.ShapeDtypeStruct((KVH, slots, rows, 2 * HD), jnp.bfloat16),
            jax.ShapeDtypeStruct((8, 128), jnp.int32),
        ],
        name="pack",
    )(routes, patch)


def judge_kernel(
    plen_ref, live_ref, tiles_ref, prefix_ref, queries_ref, suffix_ref, head_ref,
    context_ref, advantage_ref,
    *scratch,
):
    image = scratch[:KVH]
    (
        prefix, suffix, queries, keys, values, context, acc,
        routes, routes_s, scores_out, scores_in, squares_out, squares_in,
        local_sem, own_sem, out_sem, tile_send, tile_recv,
        route_send, route_recv, prefix_send, prefix_recv, relay_sem,
        score_send, score_recv, square_send, square_recv,
    ) = scratch[KVH:]
    me = lax.axis_index("slot")
    prompt = lax.axis_index("prompt")
    n_slot = lax.axis_size("slot")
    n_prompt = lax.axis_size("prompt")
    x, y, c = me // 4, (me // 2) % 2, me % 2
    chip = me // 2
    n_rows = keys.shape[0]
    n_prefix = prefix.shape[2]
    n_suffix = suffix.shape[0]
    tile = image[0].shape[1]
    n_tiles = (n_rows - n_prefix - n_suffix) // tile

    def peer(offset):
        tx = lax.rem(x + offset[0], 4)
        ty = lax.rem(y + offset[1], 2)
        tc = lax.rem(c + offset[2], 2)
        return (tx * 2 + ty) * 2 + tc

    def remote(src, dst, send, recv, **where):
        return pltpu.make_async_remote_copy(
            src, dst, send, recv, device_id=where, device_id_type=MESH
        )

    load_queries = pltpu.make_async_copy(queries_ref, queries, local_sem.at[0])
    load_suffix = pltpu.make_async_copy(suffix_ref, suffix, local_sem.at[1])
    load_prefix = pltpu.make_async_copy(prefix_ref, prefix.at[c, chip], local_sem.at[2])
    load_routes = pltpu.make_async_copy(live_ref, routes.at[me], local_sem.at[3])
    load_prefix.start()
    load_routes.start()
    barrier = pltpu.get_barrier_semaphore()
    for k in range(1, n_slot):
        pl.semaphore_signal(
            barrier, inc=1, device_id={"slot": lax.rem(me + k, n_slot)}, device_id_type=MESH
        )
    for k in range(1, n_prompt):
        pl.semaphore_signal(
            barrier, inc=1, device_id={"prompt": lax.rem(prompt + k, n_prompt)},
            device_id_type=MESH,
        )
    pl.semaphore_wait(barrier, n_slot + n_prompt - 2)

    for offset in OFFSETS:
        remote(live_ref, routes.at[me], route_send, route_recv, slot=peer(offset)).start()
    for offset in OFFSETS:
        if offset[2] == 0:
            remote(
                prefix_ref, prefix.at[c, chip], prefix_send, prefix_recv, slot=peer(offset)
            ).start()
    for g in range(KVH):
        for offset in OFFSETS:
            target = peer(offset)
            remote(
                tiles_ref.at[g, target], image[g].at[me], tile_send.at[g], tile_recv.at[g],
                slot=target,
            ).start()
    load_suffix.start()
    load_queries.start()
    for g in range(KVH):
        pltpu.make_async_copy(tiles_ref.at[g, me], image[g].at[me], own_sem.at[g]).start()

    others = prefix.at[0, pl.ds(0, n_slot // 2 - 1)]
    load_prefix.wait()
    pltpu.make_async_copy(others, others, prefix_recv).wait()
    relay = remote(
        prefix.at[c], prefix.at[c], relay_sem.at[0], relay_sem.at[1], slot=me + 1 - 2 * c
    )
    relay.start()

    load_routes.wait()
    arrived = routes.at[pl.ds(0, n_slot - 1)]
    pltpu.make_async_copy(arrived, arrived, route_recv).wait()
    fetch = pltpu.make_async_copy(routes, routes_s, local_sem.at[3])
    fetch.start()
    fetch.wait()
    index = [jnp.int32(0)] * n_tiles
    count = jnp.int32(0)
    for s in range(n_slot):
        alive = routes_s[s, 0, me]
        for j in range(n_tiles):
            index[j] = jnp.where(
                jnp.logical_and(alive > 0, count == j), jnp.int32(s), index[j]
            )
        count = count + jnp.where(alive > 0, 1, 0)

    row = lax.broadcasted_iota(jnp.int32, (n_prefix, HD), 0)
    inside = row < plen_ref[0]
    values[:n_prefix, HD:] = jnp.where(inside, 1.0, 0.0).astype(jnp.bfloat16)
    values[n_prefix:, HD:] = jnp.ones((n_rows - n_prefix, HD), jnp.bfloat16)
    acc[...] = jnp.zeros_like(acc)
    load_suffix.wait()
    load_queries.wait()
    relay.wait()

    step = math.log2(math.e) / math.sqrt(HD)
    above = n_rows - n_suffix

    def one_group(g, carry):
        k_prefix = prefix[lax.rem(g, 2), g // 2].astype(jnp.float32)
        v_prefix = prefix[lax.rem(g, 2), KVH // 2 + g // 2].astype(jnp.float32)
        inside = lax.broadcasted_iota(jnp.int32, (n_prefix, HD), 0) < plen_ref[0]
        keys[:n_prefix, :] = jnp.where(inside, k_prefix, k_prefix[0:1, :]).astype(jnp.bfloat16)
        values[:n_prefix, :HD] = jnp.where(inside, v_prefix, 0.0).astype(jnp.bfloat16)
        k_at = pl.multiple_of(g * HD, HD)
        v_at = pl.multiple_of((KVH + g) * HD, HD)
        keys[above:, :] = suffix[:, pl.ds(k_at, HD)]
        values[above:, :HD] = suffix[:, pl.ds(v_at, HD)]
        for k in range(KVH):
            @pl.when(g == k)
            def _():
                landed = image[k].at[pl.ds(0, n_slot - 1)]
                pltpu.make_async_copy(landed, landed, tile_recv.at[k]).wait()
                pltpu.make_async_copy(
                    tiles_ref.at[k, me], image[k].at[me], own_sem.at[k]
                ).wait()
                for j in range(n_tiles):
                    at = n_prefix + j * tile
                    keys[at:at + tile, :] = image[k][index[j], :, :HD]
                    values[at:at + tile, :HD] = image[k][index[j], :, HD:]

        def one_head(i, carry):
            h = g * GROUPS + i
            at = pl.multiple_of(h * HD, HD)
            scores = lax.dot_general(
                queries[:, pl.ds(at, HD)], keys[...], (((1,), (1,)), ((), ())),
                preferred_element_type=jnp.float32,
            )
            seen = scores[:, :above]
            own = scores[:, above:]
            keep = lax.broadcasted_iota(jnp.int32, own.shape, 1) <= lax.broadcasted_iota(
                jnp.int32, own.shape, 0
            )
            own = jnp.where(keep, own, NEG)
            peak = jnp.maximum(
                jnp.max(seen, axis=1, keepdims=True), jnp.max(own, axis=1, keepdims=True)
            )
            w_seen = jnp.exp2((seen - peak) * step).astype(jnp.bfloat16)
            w_own = jnp.exp2((own - peak) * step).astype(jnp.bfloat16)
            mixed = jnp.dot(
                w_seen, values[:above, :], preferred_element_type=jnp.float32
            ) + jnp.dot(w_own, values[above:, :], preferred_element_type=jnp.float32)
            rounded = (mixed[:, :HD] / mixed[:, HD:]).astype(jnp.bfloat16)
            context[:, pl.ds(at, HD)] = rounded
            acc[...] += rounded[n_suffix - 8:, :].astype(jnp.float32) * head_ref[pl.ds(h, 1), :]
            return carry

        lax.fori_loop(0, GROUPS, one_head, 0)
        at = pl.multiple_of(g * GROUPS * HD, GROUPS * HD)
        block = pl.ds(at, GROUPS * HD)
        pltpu.make_async_copy(context.at[:, block], context_ref.at[:, block], out_sem).start()
        return carry

    lax.fori_loop(0, KVH, one_group, 0)

    score = jnp.sum(acc[7:8, :], axis=1, keepdims=True)
    score = jnp.broadcast_to(score, scores_out.shape)
    scores_out[...] = score
    for offset in OFFSETS:
        remote(scores_out, scores_in.at[me], score_send, score_recv, slot=peer(offset)).start()
    scores_in[me] = score
    arrived = scores_in.at[pl.ds(0, n_slot - 1)]
    pltpu.make_async_copy(arrived, arrived, score_recv).wait()
    centre = jnp.sum(scores_in[...], axis=0) / n_slot
    deviation = scores_in[...] - centre[None]
    squares = jnp.sum(deviation * deviation, axis=0)
    squares_out[...] = squares
    for k in range(1, n_prompt):
        remote(
            squares_out, squares_in.at[prompt], square_send, square_recv,
            prompt=lax.rem(prompt + k, n_prompt),
        ).start()
    squares_in[prompt] = squares
    arrived_p = squares_in.at[pl.ds(0, n_prompt - 1)]
    pltpu.make_async_copy(arrived_p, arrived_p, square_recv).wait()
    spread = jnp.sum(squares_in[...], axis=0) / (n_slot * n_prompt)
    result = (score - centre) / jnp.sqrt(spread + 1e-06)
    advantage_ref[...] = result[0:1, 0:1]

    pltpu.make_async_copy(arrived, arrived, score_send).wait()
    pltpu.make_async_copy(arrived_p, arrived_p, square_send).wait()
    sent = routes.at[pl.ds(0, n_slot - 1)]
    pltpu.make_async_copy(sent, sent, route_send).wait()
    pltpu.make_async_copy(others, others, prefix_send).wait()
    for k in range(KVH):
        landed = image[k].at[pl.ds(0, n_slot - 1)]
        pltpu.make_async_copy(landed, landed, tile_send.at[k]).wait()
    pltpu.make_async_copy(context, context_ref, out_sem).wait()


def judge(plen, live, tiles, prefix, queries, suffix, head):
    groups, n_slot, tile, width = tiles.shape
    n_suffix, q_width = queries.shape
    n_prefix = prefix.shape[0]
    n_rows = n_prefix + n_slot // 2 * tile + n_suffix
    n_prompt = lax.axis_size("prompt")
    vmem = pl.BlockSpec(memory_space=pltpu.VMEM)
    hbm = pl.BlockSpec(memory_space=pl.ANY)
    dma = pltpu.SemaphoreType.DMA
    return pl.pallas_call(
        judge_kernel,
        in_specs=[
            pl.BlockSpec(memory_space=pltpu.SMEM), vmem, hbm, hbm, hbm, hbm, vmem,
        ],
        out_specs=[hbm, vmem],
        out_shape=[
            jax.ShapeDtypeStruct((n_suffix, q_width), jnp.bfloat16),
            jax.ShapeDtypeStruct((1, 1), jnp.float32),
        ],
        scratch_shapes=[pltpu.VMEM((n_slot, tile, width), jnp.bfloat16)] * groups + [
            pltpu.VMEM((2, n_slot // 2, n_prefix, HD), jnp.bfloat16),
            pltpu.VMEM(suffix.shape, jnp.bfloat16),
            pltpu.VMEM(queries.shape, jnp.bfloat16),
            pltpu.VMEM((n_rows, HD), jnp.bfloat16),
            pltpu.VMEM((n_rows, 2 * HD), jnp.bfloat16),
            pltpu.VMEM(queries.shape, jnp.bfloat16),
            pltpu.VMEM((8, HD), jnp.float32),
            pltpu.VMEM((n_slot, 8, 128), jnp.int32),
            pltpu.SMEM((n_slot, 8, 128), jnp.int32),
            pltpu.VMEM((8, 128), jnp.float32),
            pltpu.VMEM((n_slot, 8, 128), jnp.float32),
            pltpu.VMEM((8, 128), jnp.float32),
            pltpu.VMEM((n_prompt, 8, 128), jnp.float32),
            dma((4,)), dma((groups,)), dma(()), dma((groups,)), dma((groups,)),
            dma(()), dma(()), dma(()), dma(()), dma((2,)),
            dma(()), dma(()), dma(()), dma(()),
        ],
        compiler_params=pltpu.CompilerParams(
            collective_id=0, has_side_effects=True, vmem_limit_bytes=56 << 20
        ),
        name="judge",
    )(plen, live, tiles, prefix, queries, suffix, head)


def per_device(patch_kv, routes, prefix_kv, prefix_len, queries, suffix_kv, score_head):
    tiles, live = pack(routes, patch_kv[0])
    context, advantage = judge(
        prefix_len, live, tiles, prefix_kv[0], queries[0, 0], suffix_kv[0, 0],
        score_head.reshape(HEADS, HD),
    )
    return (context[None, None], advantage)


def solution(mesh):
    placed = (
        P("prompt", "slot", None, None),
        P("prompt", "slot"),
        P("prompt", None, "slot"),
        P("prompt"),
        P("prompt", "slot", None, None),
        P("prompt", "slot", None, None),
        P(),
    )
    return jax.shard_map(
        per_device,
        mesh=mesh,
        in_specs=placed,
        out_specs=(P("prompt", "slot", None, None), P("prompt", "slot")),
        check_vma=False,
    )
```

```python
import math

import jax
import jax.numpy as jnp
from jax import lax
from jax.experimental import pallas as pl
from jax.experimental.pallas import tpu as pltpu
from jax.sharding import PartitionSpec as P

HEADS = 64
KVH = 8
HD = 128
GROUPS = HEADS // KVH
MESH = pl.DeviceIdType.MESH
OFFSETS = (
    (1, 0, 0), (3, 0, 0), (0, 1, 0), (2, 0, 0), (1, 1, 0),
    (3, 1, 0), (0, 1, 1), (2, 1, 0), (1, 0, 1), (3, 0, 1),
    (2, 0, 1), (1, 1, 1), (3, 1, 1), (2, 1, 1), (0, 0, 1),
)
NEG = -1e30


def judge_kernel(
    plen_ref, routes_ref, patch_ref, prefix_ref, queries_ref, suffix_ref, head_ref,
    context_ref, advantage_ref,
    *scratch,
):
    image = scratch[:KVH]
    staged = scratch[KVH:2 * KVH]
    packed = scratch[2 * KVH:3 * KVH]
    (
        prefix, suffix, queries, keys, values, context, scores_a, scores_b, acc,
        live, routes, routes_s, scores_out, scores_in, squares_out, squares_in,
        local_sem, stage_sem, out_sem, tile_send, tile_recv,
        route_send, route_recv, prefix_send, prefix_recv, relay_sem,
        score_send, score_recv, square_send, square_recv,
    ) = scratch[3 * KVH:]
    me = lax.axis_index("slot")
    prompt = lax.axis_index("prompt")
    n_slot = lax.axis_size("slot")
    n_prompt = lax.axis_size("prompt")
    x, y, c = me // 4, (me // 2) % 2, me % 2
    chip = me // 2
    n_rows = keys.shape[0]
    n_prefix = prefix.shape[2]
    n_suffix = suffix.shape[0]
    tile = image[0].shape[1]
    n_tiles = (n_rows - n_prefix - n_suffix) // tile

    def peer(offset):
        tx = lax.rem(x + offset[0], 4)
        ty = lax.rem(y + offset[1], 2)
        tc = lax.rem(c + offset[2], 2)
        return (tx * 2 + ty) * 2 + tc

    def remote(src, dst, send, recv, **where):
        return pltpu.make_async_remote_copy(
            src, dst, send, recv, device_id=where, device_id_type=MESH
        )

    def stage(g):
        return [
            pltpu.make_async_copy(
                patch_ref.at[:, :, pl.ds(at * HD, HD)], staged[g].at[:, :, pl.ds(k * HD, HD)],
                stage_sem.at[g],
            )
            for k, at in enumerate((g, KVH + g))
        ]

    load_queries = pltpu.make_async_copy(queries_ref, queries, local_sem.at[0])
    load_suffix = pltpu.make_async_copy(suffix_ref, suffix, local_sem.at[1])
    load_prefix = pltpu.make_async_copy(prefix_ref, prefix.at[c, chip], local_sem.at[2])
    for g in range(KVH):
        for copy in stage(g):
            copy.start()
    load_prefix.start()
    barrier = pltpu.get_barrier_semaphore()
    for k in range(1, n_slot):
        pl.semaphore_signal(
            barrier, inc=1, device_id={"slot": lax.rem(me + k, n_slot)}, device_id_type=MESH
        )
    for k in range(1, n_prompt):
        pl.semaphore_signal(
            barrier, inc=1, device_id={"prompt": lax.rem(prompt + k, n_prompt)},
            device_id_type=MESH,
        )
    lane = lax.broadcasted_iota(jnp.int32, live.shape, 1)
    flags = jnp.zeros(live.shape, jnp.int32)
    slots = [jnp.int32(0)] * n_slot
    own_slot = jnp.int32(0)
    for k in range(n_slot):
        judge_of = routes_ref[0, k]
        flags = flags + jnp.where(lane == judge_of, 1, 0)
        own_slot = jnp.where(judge_of == me, jnp.int32(k), own_slot)
        for d in range(n_slot):
            slots[d] = jnp.where(judge_of == d, jnp.int32(k), slots[d])
    live[...] = flags
    routes[me] = flags
    pl.semaphore_wait(barrier, n_slot + n_prompt - 2)

    for offset in OFFSETS:
        if offset[2] == 0:
            remote(
                prefix_ref, prefix.at[c, chip], prefix_send, prefix_recv, slot=peer(offset)
            ).start()
    for offset in OFFSETS:
        remote(live, routes.at[me], route_send, route_recv, slot=peer(offset)).start()

    def send_tiles(g):
        for offset in OFFSETS:
            target = peer(offset)
            remote(
                packed[g].at[target], image[g].at[me], tile_send.at[g], tile_recv.at[g],
                slot=target,
            ).start()

    for g in range(KVH):
        for copy in stage(g):
            copy.wait()
        for d in range(n_slot):
            packed[g][d] = staged[g][slots[d]]
        image[g][me] = staged[g][own_slot]
        if g > 0:
            send_tiles(g - 1)
    send_tiles(KVH - 1)
    load_suffix.start()
    load_queries.start()

    others = prefix.at[0, pl.ds(0, n_slot // 2 - 1)]
    load_prefix.wait()
    pltpu.make_async_copy(others, others, prefix_recv).wait()
    relay = remote(
        prefix.at[c], prefix.at[c], relay_sem.at[0], relay_sem.at[1], slot=me + 1 - 2 * c
    )
    relay.start()

    arrived = routes.at[pl.ds(0, n_slot - 1)]
    pltpu.make_async_copy(arrived, arrived, route_recv).wait()
    fetch = pltpu.make_async_copy(routes, routes_s, local_sem.at[3])
    fetch.start()
    fetch.wait()
    index = [jnp.int32(0)] * n_tiles
    count = jnp.int32(0)
    for s in range(n_slot):
        alive = routes_s[s, 0, me]
        for j in range(n_tiles):
            index[j] = jnp.where(
                jnp.logical_and(alive > 0, count == j), jnp.int32(s), index[j]
            )
        count = count + jnp.where(alive > 0, 1, 0)

    inside = lax.broadcasted_iota(jnp.int32, (16, n_prefix), 1) < plen_ref[0]
    values[HD:, :n_prefix] = jnp.where(inside, 1.0, 0.0).astype(jnp.bfloat16)
    values[HD:, n_prefix:] = jnp.ones((16, n_rows - n_prefix), jnp.bfloat16)
    acc[...] = jnp.zeros_like(acc)
    load_suffix.wait()
    load_queries.wait()
    relay.wait()

    step = math.log2(math.e) / math.sqrt(HD)
    above = n_rows - n_suffix

    def score_head(scores, h):
        at = pl.multiple_of(h * HD, HD)
        scores[...] = lax.dot_general(
            keys[...], queries[:, pl.ds(at, HD)], (((1,), (1,)), ((), ())),
            preferred_element_type=jnp.float32,
        )

    def mix_head(scores, h):
        seen = scores[:above, :]
        own = scores[above:, :]
        keep = lax.broadcasted_iota(jnp.int32, own.shape, 0) <= lax.broadcasted_iota(
            jnp.int32, own.shape, 1
        )
        own = jnp.where(keep, own, NEG)
        peak = jnp.maximum(
            jnp.max(seen, axis=0, keepdims=True), jnp.max(own, axis=0, keepdims=True)
        )
        w_seen = jnp.exp2((seen - peak) * step).astype(jnp.bfloat16)
        w_own = jnp.exp2((own - peak) * step).astype(jnp.bfloat16)
        weights = jnp.concatenate([w_seen, w_own], axis=0)
        mixed = jnp.dot(values[...], weights, preferred_element_type=jnp.float32)
        rounded = (mixed[:HD] / mixed[HD:HD + 1]).T.astype(jnp.bfloat16)
        at = pl.multiple_of(h * HD, HD)
        context[:, pl.ds(at, HD)] = rounded
        acc[...] += rounded[n_suffix - 8:, :].astype(jnp.float32) * head_ref[pl.ds(h, 1), :]

    def one_group(g, carry):
        k_prefix = prefix[lax.rem(g, 2), g // 2].astype(jnp.float32)
        v_prefix = prefix[lax.rem(g, 2), KVH // 2 + g // 2].astype(jnp.float32)
        inside = lax.broadcasted_iota(jnp.int32, (n_prefix, HD), 0) < plen_ref[0]
        keys[:n_prefix, :] = jnp.where(inside, k_prefix, k_prefix[0:1, :]).astype(jnp.bfloat16)
        values[:HD, :n_prefix] = jnp.where(inside, v_prefix, 0.0).T.astype(jnp.bfloat16)
        k_at = pl.multiple_of(g * HD, HD)
        v_at = pl.multiple_of((KVH + g) * HD, HD)
        keys[above:, :] = suffix[:, pl.ds(k_at, HD)]
        values[:HD, above:] = suffix[:, pl.ds(v_at, HD)].T
        for k in range(KVH):
            @pl.when(g == k)
            def _():
                landed = image[k].at[pl.ds(0, n_slot - 1)]
                pltpu.make_async_copy(landed, landed, tile_recv.at[k]).wait()
                for j in range(n_tiles):
                    at = n_prefix + j * tile
                    keys[at:at + tile, :] = image[k][index[j], :, :HD]
                    values[:HD, at:at + tile] = image[k][index[j], :, HD:].T

        first = g * GROUPS
        last = first + GROUPS - 1
        score_head(scores_a, first)

        def two_heads(i, carry):
            h = first + 2 * i
            score_head(scores_b, h + 1)
            mix_head(scores_a, h)
            score_head(scores_a, jnp.minimum(h + 2, last))
            mix_head(scores_b, h + 1)
            return carry

        lax.fori_loop(0, GROUPS // 2, two_heads, 0)
        at = pl.multiple_of(g * GROUPS * HD, GROUPS * HD)
        block = pl.ds(at, GROUPS * HD)
        pltpu.make_async_copy(context.at[:, block], context_ref.at[:, block], out_sem).start()
        return carry

    lax.fori_loop(0, KVH, one_group, 0)

    score = jnp.sum(acc[7:8, :], axis=1, keepdims=True)
    score = jnp.broadcast_to(score, scores_out.shape)
    scores_out[...] = score
    for offset in OFFSETS:
        remote(scores_out, scores_in.at[me], score_send, score_recv, slot=peer(offset)).start()
    scores_in[me] = score
    arrived = scores_in.at[pl.ds(0, n_slot - 1)]
    pltpu.make_async_copy(arrived, arrived, score_recv).wait()
    centre = jnp.sum(scores_in[...], axis=0) / n_slot
    deviation = scores_in[...] - centre[None]
    squares = jnp.sum(deviation * deviation, axis=0)
    squares_out[...] = squares
    for k in range(1, n_prompt):
        remote(
            squares_out, squares_in.at[prompt], square_send, square_recv,
            prompt=lax.rem(prompt + k, n_prompt),
        ).start()
    squares_in[prompt] = squares
    arrived_p = squares_in.at[pl.ds(0, n_prompt - 1)]
    pltpu.make_async_copy(arrived_p, arrived_p, square_recv).wait()
    spread = jnp.sum(squares_in[...], axis=0) / (n_slot * n_prompt)
    result = (score - centre) / jnp.sqrt(spread + 1e-06)
    advantage_ref[...] = result[0:1, 0:1]

    pltpu.make_async_copy(arrived, arrived, score_send).wait()
    pltpu.make_async_copy(arrived_p, arrived_p, square_send).wait()
    sent = routes.at[pl.ds(0, n_slot - 1)]
    pltpu.make_async_copy(sent, sent, route_send).wait()
    pltpu.make_async_copy(others, others, prefix_send).wait()
    for k in range(KVH):
        landed = image[k].at[pl.ds(0, n_slot - 1)]
        pltpu.make_async_copy(landed, landed, tile_send.at[k]).wait()
    pltpu.make_async_copy(context, context_ref, out_sem).wait()


def judge(plen, routes, patch, prefix, queries, suffix, head):
    n_slot, tile, width = patch.shape
    n_suffix, q_width = queries.shape
    n_prefix = prefix.shape[0]
    n_rows = n_prefix + n_slot // 2 * tile + n_suffix
    n_prompt = lax.axis_size("prompt")
    vmem = pl.BlockSpec(memory_space=pltpu.VMEM)
    smem = pl.BlockSpec(memory_space=pltpu.SMEM)
    hbm = pl.BlockSpec(memory_space=pl.ANY)
    dma = pltpu.SemaphoreType.DMA
    return pl.pallas_call(
        judge_kernel,
        in_specs=[smem, smem, hbm, hbm, hbm, hbm, vmem],
        out_specs=[hbm, vmem],
        out_shape=[
            jax.ShapeDtypeStruct((n_suffix, q_width), jnp.bfloat16),
            jax.ShapeDtypeStruct((1, 1), jnp.float32),
        ],
        scratch_shapes=[pltpu.VMEM((n_slot, tile, 2 * HD), jnp.bfloat16)] * (3 * KVH) + [
            pltpu.VMEM((2, n_slot // 2, n_prefix, HD), jnp.bfloat16),
            pltpu.VMEM(suffix.shape, jnp.bfloat16),
            pltpu.VMEM(queries.shape, jnp.bfloat16),
            pltpu.VMEM((n_rows, HD), jnp.bfloat16),
            pltpu.VMEM((HD + 16, n_rows), jnp.bfloat16),
            pltpu.VMEM(queries.shape, jnp.bfloat16),
            pltpu.VMEM((n_rows, n_suffix), jnp.float32),
            pltpu.VMEM((n_rows, n_suffix), jnp.float32),
            pltpu.VMEM((8, HD), jnp.float32),
            pltpu.VMEM((8, 128), jnp.int32),
            pltpu.VMEM((n_slot, 8, 128), jnp.int32),
            pltpu.SMEM((n_slot, 8, 128), jnp.int32),
            pltpu.VMEM((8, 128), jnp.float32),
            pltpu.VMEM((n_slot, 8, 128), jnp.float32),
            pltpu.VMEM((8, 128), jnp.float32),
            pltpu.VMEM((n_prompt, 8, 128), jnp.float32),
            dma((4,)), dma((KVH,)), dma(()), dma((KVH,)), dma((KVH,)),
            dma(()), dma(()), dma(()), dma(()), dma((2,)),
            dma(()), dma(()), dma(()), dma(()),
        ],
        compiler_params=pltpu.CompilerParams(
            collective_id=0, has_side_effects=True, vmem_limit_bytes=58 << 20
        ),
        name="judge",
    )(plen, routes, patch, prefix, queries, suffix, head)


def per_device(patch_kv, routes, prefix_kv, prefix_len, queries, suffix_kv, score_head):
    context, advantage = judge(
        prefix_len, routes, patch_kv[0], prefix_kv[0], queries[0, 0], suffix_kv[0, 0],
        score_head.reshape(HEADS, HD),
    )
    return (context[None, None], advantage)


def solution(mesh):
    placed = (
        P("prompt", "slot", None, None),
        P("prompt", "slot"),
        P("prompt", None, "slot"),
        P("prompt"),
        P("prompt", "slot", None, None),
        P("prompt", "slot", None, None),
        P(),
    )
    return jax.shard_map(
        per_device,
        mesh=mesh,
        in_specs=placed,
        out_specs=(P("prompt", "slot", None, None), P("prompt", "slot")),
        check_vma=False,
    )
```

```python
import math

import jax
import jax.numpy as jnp
from jax import lax
from jax.experimental import pallas as pl
from jax.experimental.pallas import tpu as pltpu
from jax.sharding import PartitionSpec as P

HEADS = 64
KVH = 8
HD = 128
GROUPS = HEADS // KVH
MESH = pl.DeviceIdType.MESH
OFFSETS = (
    (1, 0, 0), (3, 0, 0), (0, 1, 0), (2, 0, 0), (1, 1, 0),
    (3, 1, 0), (0, 1, 1), (2, 1, 0), (1, 0, 1), (3, 0, 1),
    (2, 0, 1), (1, 1, 1), (3, 1, 1), (2, 1, 1), (0, 0, 1),
)
NEG = -1e30


def judge_kernel(
    plen_ref, routes_ref, patch_ref, prefix_ref, queries_ref, suffix_ref, head_ref,
    context, advantage_ref,
    *scratch,
):
    image = scratch[:KVH]
    staged = scratch[KVH:2 * KVH]
    packed = scratch[2 * KVH:3 * KVH]
    (
        prefix, suffix, queries, keys, values, scores_a, scores_b, acc,
        live, routes, routes_s, scores_out, scores_in, squares_out, squares_in,
        local_sem, stage_sem, tile_send, tile_recv,
        route_send, route_recv, prefix_send, prefix_recv, relay_sem,
        score_send, score_recv, square_send, square_recv,
    ) = scratch[3 * KVH:]
    me = lax.axis_index("slot")
    prompt = lax.axis_index("prompt")
    n_slot = lax.axis_size("slot")
    n_prompt = lax.axis_size("prompt")
    x, y, c = me // 4, (me // 2) % 2, me % 2
    chip = me // 2
    n_rows = keys.shape[0]
    n_prefix = prefix.shape[2]
    n_suffix = suffix.shape[0]
    tile = image[0].shape[1]
    n_tiles = (n_rows - n_prefix - n_suffix) // tile

    def peer(offset):
        tx = lax.rem(x + offset[0], 4)
        ty = lax.rem(y + offset[1], 2)
        tc = lax.rem(c + offset[2], 2)
        return (tx * 2 + ty) * 2 + tc

    def remote(src, dst, send, recv, **where):
        return pltpu.make_async_remote_copy(
            src, dst, send, recv, device_id=where, device_id_type=MESH
        )

    def stage(g):
        return [
            pltpu.make_async_copy(
                patch_ref.at[:, :, pl.ds(at * HD, HD)], staged[g].at[:, :, pl.ds(k * HD, HD)],
                stage_sem.at[g],
            )
            for k, at in enumerate((g, KVH + g))
        ]

    load_queries = pltpu.make_async_copy(queries_ref, queries, local_sem.at[0])
    load_suffix = pltpu.make_async_copy(suffix_ref, suffix, local_sem.at[1])
    load_prefix = pltpu.make_async_copy(prefix_ref, prefix.at[c, chip], local_sem.at[2])
    for copy in stage(0) + stage(1):
        copy.start()
    load_prefix.start()
    barrier = pltpu.get_barrier_semaphore()
    for k in range(1, n_slot):
        pl.semaphore_signal(
            barrier, inc=1, device_id={"slot": lax.rem(me + k, n_slot)}, device_id_type=MESH
        )
    for k in range(1, n_prompt):
        pl.semaphore_signal(
            barrier, inc=1, device_id={"prompt": lax.rem(prompt + k, n_prompt)},
            device_id_type=MESH,
        )
    lane = lax.broadcasted_iota(jnp.int32, live.shape, 1)
    flags = jnp.zeros(live.shape, jnp.int32)
    slots = [jnp.int32(0)] * n_slot
    own_slot = jnp.int32(0)
    for k in range(n_slot):
        judge_of = routes_ref[0, k]
        flags = flags + jnp.where(lane == judge_of, 1, 0)
        own_slot = jnp.where(judge_of == me, jnp.int32(k), own_slot)
        for d in range(n_slot):
            slots[d] = jnp.where(judge_of == d, jnp.int32(k), slots[d])
    live[...] = flags
    routes[me] = flags
    pl.semaphore_wait(barrier, n_slot + n_prompt - 2)

    for offset in OFFSETS:
        if offset[2] == 0:
            remote(
                prefix_ref, prefix.at[c, chip], prefix_send, prefix_recv, slot=peer(offset)
            ).start()
    for offset in OFFSETS:
        remote(live, routes.at[me], route_send, route_recv, slot=peer(offset)).start()

    def send_tiles(g):
        for offset in OFFSETS:
            target = peer(offset)
            remote(
                packed[g].at[target], image[g].at[me], tile_send.at[g], tile_recv.at[g],
                slot=target,
            ).start()

    for g in range(KVH):
        for copy in stage(g):
            copy.wait()
        if g + 2 < KVH:
            for copy in stage(g + 2):
                copy.start()
        for d in range(n_slot):
            packed[g][d] = staged[g][slots[d]]
        image[g][me] = staged[g][own_slot]
        if g > 0:
            send_tiles(g - 1)
    send_tiles(KVH - 1)
    load_suffix.start()
    load_queries.start()

    others = prefix.at[0, pl.ds(0, n_slot // 2 - 1)]
    load_prefix.wait()
    pltpu.make_async_copy(others, others, prefix_recv).wait()
    relay = remote(
        prefix.at[c], prefix.at[c], relay_sem.at[0], relay_sem.at[1], slot=me + 1 - 2 * c
    )
    relay.start()

    arrived = routes.at[pl.ds(0, n_slot - 1)]
    pltpu.make_async_copy(arrived, arrived, route_recv).wait()
    fetch = pltpu.make_async_copy(routes, routes_s, local_sem.at[3])
    fetch.start()
    fetch.wait()
    index = [jnp.int32(0)] * n_tiles
    count = jnp.int32(0)
    for s in range(n_slot):
        alive = routes_s[s, 0, me]
        for j in range(n_tiles):
            index[j] = jnp.where(
                jnp.logical_and(alive > 0, count == j), jnp.int32(s), index[j]
            )
        count = count + jnp.where(alive > 0, 1, 0)

    inside = lax.broadcasted_iota(jnp.int32, (16, n_prefix), 1) < plen_ref[0]
    values[HD:, :n_prefix] = jnp.where(inside, 1.0, 0.0).astype(jnp.bfloat16)
    values[HD:, n_prefix:] = jnp.ones((16, n_rows - n_prefix), jnp.bfloat16)
    acc[...] = jnp.zeros_like(acc)
    load_suffix.wait()
    load_queries.wait()
    relay.wait()

    step = math.log2(math.e) / math.sqrt(HD)
    above = n_rows - n_suffix

    def add_score(rows, h):
        acc[...] += rows.astype(jnp.float32) * head_ref[pl.ds(h, 1), :]

    def score_last_rows(first):
        tail = jnp.concatenate(
            [
                queries[n_suffix - 16:, (first + i) * HD:(first + i + 1) * HD]
                for i in range(GROUPS)
            ],
            axis=0,
        )
        scores = lax.dot_general(
            keys[...], tail, (((1,), (1,)), ((), ())), preferred_element_type=jnp.float32
        )
        peak = jnp.max(scores, axis=0, keepdims=True)
        weights = jnp.exp2((scores - peak) * step).astype(jnp.bfloat16)
        mixed = jnp.dot(values[...], weights, preferred_element_type=jnp.float32)
        rounded = (mixed[:HD] / mixed[HD:HD + 1]).T.astype(jnp.bfloat16)
        for i in range(GROUPS):
            add_score(rounded[16 * i + 8:16 * i + 16, :], first + i)

    def score_head(scores, h):
        at = pl.multiple_of(h * HD, HD)
        scores[...] = lax.dot_general(
            keys[...], queries[:, pl.ds(at, HD)], (((1,), (1,)), ((), ())),
            preferred_element_type=jnp.float32,
        )

    def mix_head(scores, h, score):
        seen = scores[:above, :]
        own = scores[above:, :]
        keep = lax.broadcasted_iota(jnp.int32, own.shape, 0) <= lax.broadcasted_iota(
            jnp.int32, own.shape, 1
        )
        own = jnp.where(keep, own, NEG)
        peak = jnp.maximum(
            jnp.max(seen, axis=0, keepdims=True), jnp.max(own, axis=0, keepdims=True)
        )
        w_seen = jnp.exp2((seen - peak) * step).astype(jnp.bfloat16)
        w_own = jnp.exp2((own - peak) * step).astype(jnp.bfloat16)
        weights = jnp.concatenate([w_seen, w_own], axis=0)
        mixed = jnp.dot(values[...], weights, preferred_element_type=jnp.float32)
        rounded = (mixed[:HD] / mixed[HD:HD + 1]).T.astype(jnp.bfloat16)
        at = pl.multiple_of(h * HD, HD)
        context[:, pl.ds(at, HD)] = rounded
        if score:
            add_score(rounded[n_suffix - 8:, :], h)

    def build(g, pieces):
        k_prefix = prefix[lax.rem(g, 2), g // 2].astype(jnp.float32)
        v_prefix = prefix[lax.rem(g, 2), KVH // 2 + g // 2].astype(jnp.float32)
        inside = lax.broadcasted_iota(jnp.int32, (n_prefix, HD), 0) < plen_ref[0]
        keys[:n_prefix, :] = jnp.where(inside, k_prefix, k_prefix[0:1, :]).astype(jnp.bfloat16)
        values[:HD, :n_prefix] = jnp.where(inside, v_prefix, 0.0).T.astype(jnp.bfloat16)
        k_at = pl.multiple_of(g * HD, HD)
        v_at = pl.multiple_of((KVH + g) * HD, HD)
        keys[above:, :] = suffix[:, pl.ds(k_at, HD)]
        values[:HD, above:] = suffix[:, pl.ds(v_at, HD)].T
        for k in pieces:
            @pl.when(g == k)
            def _():
                landed = image[k].at[pl.ds(0, n_slot - 1)]
                pltpu.make_async_copy(landed, landed, tile_recv.at[k]).wait()
                for j in range(n_tiles):
                    at = n_prefix + j * tile
                    keys[at:at + tile, :] = image[k][index[j], :, :HD]
                    values[:HD, at:at + tile] = image[k][index[j], :, HD:].T


    def two_heads(first, i, score):
        last = first + GROUPS - 1
        h = first + 2 * i
        score_head(scores_b, h + 1)
        mix_head(scores_a, h, score)
        score_head(scores_a, jnp.minimum(h + 2, last))
        mix_head(scores_b, h + 1, score)

    def one_group(g, carry):
        build(g, range(KVH - 1))
        first = g * GROUPS
        score_head(scores_a, first)

        def body(i, carry):
            two_heads(first, i, True)
            return carry

        lax.fori_loop(0, GROUPS // 2, body, 0)
        return carry

    lax.fori_loop(0, KVH - 1, one_group, 0)

    final = KVH - 1
    build(final, [final])
    score_last_rows(final * GROUPS)
    score = jnp.sum(acc[7:8, :], axis=1, keepdims=True)
    score = jnp.broadcast_to(score, scores_out.shape)
    scores_out[...] = score
    for offset in OFFSETS:
        remote(scores_out, scores_in.at[me], score_send, score_recv, slot=peer(offset)).start()
    scores_in[me] = score
    score_head(scores_a, final * GROUPS)

    def early(i, carry):
        two_heads(final * GROUPS, i, False)
        return carry

    lax.fori_loop(0, GROUPS // 4, early, 0)
    arrived = scores_in.at[pl.ds(0, n_slot - 1)]
    pltpu.make_async_copy(arrived, arrived, score_recv).wait()
    centre = jnp.sum(scores_in[...], axis=0) / n_slot
    deviation = scores_in[...] - centre[None]
    squares = jnp.sum(deviation * deviation, axis=0)
    squares_out[...] = squares
    for k in range(1, n_prompt):
        remote(
            squares_out, squares_in.at[prompt], square_send, square_recv,
            prompt=lax.rem(prompt + k, n_prompt),
        ).start()
    squares_in[prompt] = squares
    lax.fori_loop(GROUPS // 4, GROUPS // 2, early, 0)
    arrived_p = squares_in.at[pl.ds(0, n_prompt - 1)]
    pltpu.make_async_copy(arrived_p, arrived_p, square_recv).wait()
    spread = jnp.sum(squares_in[...], axis=0) / (n_slot * n_prompt)
    result = (score - centre) / jnp.sqrt(spread + 1e-06)
    advantage_ref[...] = result[0:1, 0:1]

    pltpu.make_async_copy(arrived, arrived, score_send).wait()
    pltpu.make_async_copy(arrived_p, arrived_p, square_send).wait()
    sent = routes.at[pl.ds(0, n_slot - 1)]
    pltpu.make_async_copy(sent, sent, route_send).wait()
    pltpu.make_async_copy(others, others, prefix_send).wait()
    for k in range(KVH):
        landed = image[k].at[pl.ds(0, n_slot - 1)]
        pltpu.make_async_copy(landed, landed, tile_send.at[k]).wait()


def judge(plen, routes, patch, prefix, queries, suffix, head):
    n_slot, tile, width = patch.shape
    n_suffix, q_width = queries.shape
    n_prefix = prefix.shape[0]
    n_rows = n_prefix + n_slot // 2 * tile + n_suffix
    n_prompt = lax.axis_size("prompt")
    vmem = pl.BlockSpec(memory_space=pltpu.VMEM)
    smem = pl.BlockSpec(memory_space=pltpu.SMEM)
    hbm = pl.BlockSpec(memory_space=pl.ANY)
    dma = pltpu.SemaphoreType.DMA
    return pl.pallas_call(
        judge_kernel,
        in_specs=[smem, smem, hbm, hbm, hbm, hbm, vmem],
        out_specs=[vmem, vmem],
        out_shape=[
            pltpu.VMEM((n_suffix, q_width), jnp.bfloat16),
            jax.ShapeDtypeStruct((1, 1), jnp.float32),
        ],
        scratch_shapes=[pltpu.VMEM((n_slot, tile, 2 * HD), jnp.bfloat16)] * (3 * KVH) + [
            pltpu.VMEM((2, n_slot // 2, n_prefix, HD), jnp.bfloat16),
            pltpu.VMEM(suffix.shape, jnp.bfloat16),
            pltpu.VMEM(queries.shape, jnp.bfloat16),
            pltpu.VMEM((n_rows, HD), jnp.bfloat16),
            pltpu.VMEM((HD + 16, n_rows), jnp.bfloat16),
            pltpu.VMEM((n_rows, n_suffix), jnp.float32),
            pltpu.VMEM((n_rows, n_suffix), jnp.float32),
            pltpu.VMEM((8, HD), jnp.float32),
            pltpu.VMEM((8, 128), jnp.int32),
            pltpu.VMEM((n_slot, 8, 128), jnp.int32),
            pltpu.SMEM((n_slot, 8, 128), jnp.int32),
            pltpu.VMEM((8, 128), jnp.float32),
            pltpu.VMEM((n_slot, 8, 128), jnp.float32),
            pltpu.VMEM((8, 128), jnp.float32),
            pltpu.VMEM((n_prompt, 8, 128), jnp.float32),
            dma((4,)), dma((KVH,)), dma((KVH,)), dma((KVH,)),
            dma(()), dma(()), dma(()), dma(()), dma((2,)),
            dma(()), dma(()), dma(()), dma(()),
        ],
        compiler_params=pltpu.CompilerParams(
            collective_id=0, has_side_effects=True, vmem_limit_bytes=52 << 20
        ),
        name="judge",
    )(plen, routes, patch, prefix, queries, suffix, head)


def per_device(patch_kv, routes, prefix_kv, prefix_len, queries, suffix_kv, score_head):
    context, advantage = judge(
        prefix_len, routes, patch_kv[0], prefix_kv[0], queries[0, 0], suffix_kv[0, 0],
        score_head.reshape(HEADS, HD),
    )
    return (context[None, None], advantage)


def solution(mesh):
    placed = (
        P("prompt", "slot", None, None),
        P("prompt", "slot"),
        P("prompt", None, "slot"),
        P("prompt"),
        P("prompt", "slot", None, None),
        P("prompt", "slot", None, None),
        P(),
    )
    return jax.shard_map(
        per_device,
        mesh=mesh,
        in_specs=placed,
        out_specs=(P("prompt", "slot", None, None), P("prompt", "slot")),
        check_vma=False,
    )
```

```python
import math

import jax
import jax.numpy as jnp
from jax import lax
from jax.experimental import pallas as pl
from jax.experimental.pallas import tpu as pltpu
from jax.sharding import PartitionSpec as P

HEADS = 64
KVH = 8
HD = 128
GROUPS = HEADS // KVH
MESH = pl.DeviceIdType.MESH
OFFSETS = (
    (1, 0, 0), (3, 0, 0), (0, 1, 0), (2, 0, 0), (1, 1, 0),
    (3, 1, 0), (0, 1, 1), (2, 1, 0), (1, 0, 1), (3, 0, 1),
    (2, 0, 1), (1, 1, 1), (3, 1, 1), (2, 1, 1), (0, 0, 1),
)
NEG = -1e30


def judge_kernel(
    plen_ref, routes_ref, patch_ref, prefix_ref, queries_ref, suffix_ref, head_ref,
    context, advantage_ref,
    *scratch,
):
    image = scratch[:KVH]
    staged = scratch[KVH:2 * KVH]
    packed = scratch[2 * KVH:3 * KVH]
    (
        prefix, suffix, queries, keys, values, scores_a, scores_b, acc,
        live, routes, routes_s, scores_out, scores_in, squares_out, squares_in,
        local_sem, stage_sem, tile_send, tile_recv,
        route_send, route_recv, prefix_send, prefix_recv, relay_sem,
        score_send, score_recv, square_send, square_recv,
    ) = scratch[3 * KVH:]
    me = lax.axis_index("slot")
    prompt = lax.axis_index("prompt")
    n_slot = lax.axis_size("slot")
    n_prompt = lax.axis_size("prompt")
    x, y, c = me // 4, (me // 2) % 2, me % 2
    n_rows = keys.shape[0]
    n_prefix = prefix.shape[3]
    n_suffix = suffix.shape[0]
    tile = image[0].shape[1]
    n_tiles = (n_rows - n_prefix - n_suffix) // tile

    def peer(offset):
        tx = lax.rem(x + offset[0], 4)
        ty = lax.rem(y + offset[1], 2)
        tc = lax.rem(c + offset[2], 2)
        return (tx * 2 + ty) * 2 + tc

    def remote(src, dst, send, recv, **where):
        return pltpu.make_async_remote_copy(
            src, dst, send, recv, device_id=where, device_id_type=MESH
        )

    def stage(g):
        return [
            pltpu.make_async_copy(
                patch_ref.at[:, :, pl.ds(at * HD, HD)], staged[g].at[:, :, pl.ds(k * HD, HD)],
                stage_sem.at[g],
            )
            for k, at in enumerate((g, KVH + g))
        ]

    load_queries = pltpu.make_async_copy(queries_ref, queries, local_sem.at[0])
    load_suffix = pltpu.make_async_copy(suffix_ref, suffix, local_sem.at[1])
    load_prefix = pltpu.make_async_copy(prefix_ref, prefix.at[c, x, y], local_sem.at[2])
    for copy in stage(0) + stage(1):
        copy.start()
    load_prefix.start()
    barrier = pltpu.get_barrier_semaphore()
    for k in range(1, n_slot):
        pl.semaphore_signal(
            barrier, inc=1, device_id={"slot": lax.rem(me + k, n_slot)}, device_id_type=MESH
        )
    for k in range(1, n_prompt):
        pl.semaphore_signal(
            barrier, inc=1, device_id={"prompt": lax.rem(prompt + k, n_prompt)},
            device_id_type=MESH,
        )
    lane = lax.broadcasted_iota(jnp.int32, live.shape, 1)
    flags = jnp.zeros(live.shape, jnp.int32)
    slots = [jnp.int32(0)] * n_slot
    own_slot = jnp.int32(0)
    for k in range(n_slot):
        judge_of = routes_ref[0, k]
        flags = flags + jnp.where(lane == judge_of, 1, 0)
        own_slot = jnp.where(judge_of == me, jnp.int32(k), own_slot)
        for d in range(n_slot):
            slots[d] = jnp.where(judge_of == d, jnp.int32(k), slots[d])
    live[...] = flags
    routes[me] = flags
    pl.semaphore_wait(barrier, n_slot + n_prompt - 2)

    cut = n_prefix * 13 // 32
    partner = peer((0, 1, 0))
    along = [peer((k, 0, 0)) for k in (1, 3, 2)]
    for target in along:
        remote(
            prefix_ref, prefix.at[c, x, y], prefix_send.at[0], prefix_recv.at[0], slot=target
        ).start()
    remote(
        prefix_ref.at[pl.ds(0, cut)], prefix.at[c, x, y, pl.ds(0, cut)],
        prefix_send.at[1], prefix_recv.at[1], slot=partner,
    ).start()
    for offset in OFFSETS:
        remote(live, routes.at[me], route_send, route_recv, slot=peer(offset)).start()
    whole = prefix.at[0, pl.ds(0, 3), 0]
    below = prefix.at[0, 0, 0, pl.ds(0, cut)]
    belows = prefix.at[0, pl.ds(0, 3), 0, pl.ds(0, cut)]
    rests = prefix.at[c, :, y, pl.ds(cut, n_prefix - cut)]

    def pass_prefix():
        load_prefix.wait()
        pltpu.make_async_copy(below, below, prefix_recv.at[1]).wait()
        theirs = prefix.at[c, x, 1 - y, pl.ds(0, cut)]
        for target in along:
            remote(
                theirs, theirs, prefix_send.at[2], prefix_recv.at[2], slot=target
            ).start()
        pltpu.make_async_copy(whole, whole, prefix_recv.at[0]).wait()
        remote(rests, rests, prefix_send.at[3], prefix_recv.at[3], slot=partner).start()

    def send_tiles(g):
        for offset in OFFSETS:
            target = peer(offset)
            remote(
                packed[g].at[target], image[g].at[me], tile_send.at[g], tile_recv.at[g],
                slot=target,
            ).start()

    for g in range(KVH):
        for copy in stage(g):
            copy.wait()
        if g + 2 < KVH:
            for copy in stage(g + 2):
                copy.start()
        for d in range(n_slot):
            packed[g][d] = staged[g][slots[d]]
        image[g][me] = staged[g][own_slot]
        if g > 0:
            send_tiles(g - 1)
        if g == 1:
            pass_prefix()
    send_tiles(KVH - 1)
    load_suffix.start()
    load_queries.start()

    pltpu.make_async_copy(belows, belows, prefix_recv.at[2]).wait()
    pltpu.make_async_copy(rests, rests, prefix_recv.at[3]).wait()
    relay = remote(
        prefix.at[c], prefix.at[c], relay_sem.at[0], relay_sem.at[1], slot=me + 1 - 2 * c
    )
    relay.start()

    arrived = routes.at[pl.ds(0, n_slot - 1)]
    pltpu.make_async_copy(arrived, arrived, route_recv).wait()
    fetch = pltpu.make_async_copy(routes, routes_s, local_sem.at[3])
    fetch.start()
    fetch.wait()
    index = [jnp.int32(0)] * n_tiles
    count = jnp.int32(0)
    for s in range(n_slot):
        alive = routes_s[s, 0, me]
        for j in range(n_tiles):
            index[j] = jnp.where(
                jnp.logical_and(alive > 0, count == j), jnp.int32(s), index[j]
            )
        count = count + jnp.where(alive > 0, 1, 0)

    inside = lax.broadcasted_iota(jnp.int32, (16, n_prefix), 1) < plen_ref[0]
    values[HD:, :n_prefix] = jnp.where(inside, 1.0, 0.0).astype(jnp.bfloat16)
    values[HD:, n_prefix:] = jnp.ones((16, n_rows - n_prefix), jnp.bfloat16)
    acc[...] = jnp.zeros_like(acc)
    load_suffix.wait()
    load_queries.wait()
    relay.wait()

    step = math.log2(math.e) / math.sqrt(HD)
    above = n_rows - n_suffix

    def add_score(rows, h):
        acc[...] += rows.astype(jnp.float32) * head_ref[pl.ds(h, 1), :]

    def score_last_rows(first):
        tail = jnp.concatenate(
            [
                queries[n_suffix - 16:, (first + i) * HD:(first + i + 1) * HD]
                for i in range(GROUPS)
            ],
            axis=0,
        )
        scores = lax.dot_general(
            keys[...], tail, (((1,), (1,)), ((), ())), preferred_element_type=jnp.float32
        )
        peak = jnp.max(scores, axis=0, keepdims=True)
        weights = jnp.exp2((scores - peak) * step).astype(jnp.bfloat16)
        mixed = jnp.dot(values[...], weights, preferred_element_type=jnp.float32)
        rounded = (mixed[:HD] / mixed[HD:HD + 1]).T.astype(jnp.bfloat16)
        for i in range(GROUPS):
            add_score(rounded[16 * i + 8:16 * i + 16, :], first + i)

    def score_head(scores, h):
        at = pl.multiple_of(h * HD, HD)
        query = queries[:, pl.ds(at, HD)]
        for rows in (pl.ds(0, n_rows // 2), pl.ds(n_rows // 2, n_rows // 2)):
            scores[rows, :] = lax.dot_general(
                keys[rows, :], query, (((1,), (1,)), ((), ())),
                preferred_element_type=jnp.float32,
            )

    def mix_head(scores, h, score):
        seen = scores[:above, :]
        own = scores[above:, :]
        keep = lax.broadcasted_iota(jnp.int32, own.shape, 0) <= lax.broadcasted_iota(
            jnp.int32, own.shape, 1
        )
        own = jnp.where(keep, own, NEG)
        peak = jnp.maximum(
            jnp.max(seen, axis=0, keepdims=True), jnp.max(own, axis=0, keepdims=True)
        )
        w_seen = jnp.exp2((seen - peak) * step).astype(jnp.bfloat16)
        w_own = jnp.exp2((own - peak) * step).astype(jnp.bfloat16)
        weights = jnp.concatenate([w_seen, w_own], axis=0)
        mixed = jnp.dot(values[...], weights, preferred_element_type=jnp.float32)
        rounded = (mixed[:HD] / mixed[HD:HD + 1]).T.astype(jnp.bfloat16)
        at = pl.multiple_of(h * HD, HD)
        context[:, pl.ds(at, HD)] = rounded
        if score:
            add_score(rounded[n_suffix - 8:, :], h)

    def build(g, pieces):
        k_prefix = prefix[lax.rem(g, 2), g // 4, lax.rem(g // 2, 2)].astype(jnp.float32)
        v_prefix = prefix[lax.rem(g, 2), 2 + g // 4, lax.rem(g // 2, 2)].astype(jnp.float32)
        inside = lax.broadcasted_iota(jnp.int32, (n_prefix, HD), 0) < plen_ref[0]
        keys[:n_prefix, :] = jnp.where(inside, k_prefix, k_prefix[0:1, :]).astype(jnp.bfloat16)
        values[:HD, :n_prefix] = jnp.where(inside, v_prefix, 0.0).T.astype(jnp.bfloat16)
        k_at = pl.multiple_of(g * HD, HD)
        v_at = pl.multiple_of((KVH + g) * HD, HD)
        keys[above:, :] = suffix[:, pl.ds(k_at, HD)]
        values[:HD, above:] = suffix[:, pl.ds(v_at, HD)].T
        for k in pieces:
            @pl.when(g == k)
            def _():
                landed = image[k].at[pl.ds(0, n_slot - 1)]
                pltpu.make_async_copy(landed, landed, tile_recv.at[k]).wait()
                for j in range(n_tiles):
                    at = n_prefix + j * tile
                    keys[at:at + tile, :] = image[k][index[j], :, :HD]
                    values[:HD, at:at + tile] = image[k][index[j], :, HD:].T


    def two_heads(first, i, score):
        last = first + GROUPS - 1
        h = first + 2 * i
        score_head(scores_b, h + 1)
        mix_head(scores_a, h, score)
        score_head(scores_a, jnp.minimum(h + 2, last))
        mix_head(scores_b, h + 1, score)

    def one_group(g, carry):
        build(g, range(KVH - 1))
        first = g * GROUPS
        score_head(scores_a, first)

        def body(i, carry):
            two_heads(first, i, True)
            return carry

        lax.fori_loop(0, GROUPS // 2, body, 0)
        return carry

    lax.fori_loop(0, KVH - 1, one_group, 0)

    final = KVH - 1
    build(final, [final])
    score_last_rows(final * GROUPS)
    score = jnp.sum(acc[7:8, :], axis=1, keepdims=True)
    score = jnp.broadcast_to(score, scores_out.shape)
    scores_out[...] = score
    for offset in OFFSETS:
        remote(scores_out, scores_in.at[me], score_send, score_recv, slot=peer(offset)).start()
    scores_in[me] = score
    score_head(scores_a, final * GROUPS)

    def early(i, carry):
        two_heads(final * GROUPS, i, False)
        return carry

    lax.fori_loop(0, GROUPS // 4, early, 0)
    arrived = scores_in.at[pl.ds(0, n_slot - 1)]
    pltpu.make_async_copy(arrived, arrived, score_recv).wait()
    centre = jnp.sum(scores_in[...], axis=0) / n_slot
    deviation = scores_in[...] - centre[None]
    squares = jnp.sum(deviation * deviation, axis=0)
    squares_out[...] = squares
    for k in range(1, n_prompt):
        remote(
            squares_out, squares_in.at[prompt], square_send, square_recv,
            prompt=lax.rem(prompt + k, n_prompt),
        ).start()
    squares_in[prompt] = squares
    lax.fori_loop(GROUPS // 4, GROUPS // 2, early, 0)
    arrived_p = squares_in.at[pl.ds(0, n_prompt - 1)]
    pltpu.make_async_copy(arrived_p, arrived_p, square_recv).wait()
    spread = jnp.sum(squares_in[...], axis=0) / (n_slot * n_prompt)
    result = (score - centre) / jnp.sqrt(spread + 1e-06)
    advantage_ref[...] = result[0:1, 0:1]

    pltpu.make_async_copy(arrived, arrived, score_send).wait()
    pltpu.make_async_copy(arrived_p, arrived_p, square_send).wait()
    sent = routes.at[pl.ds(0, n_slot - 1)]
    pltpu.make_async_copy(sent, sent, route_send).wait()
    for k, done in enumerate((whole, below, belows, rests)):
        pltpu.make_async_copy(done, done, prefix_send.at[k]).wait()
    for k in range(KVH):
        landed = image[k].at[pl.ds(0, n_slot - 1)]
        pltpu.make_async_copy(landed, landed, tile_send.at[k]).wait()


def judge(plen, routes, patch, prefix, queries, suffix, head):
    n_slot, tile, width = patch.shape
    n_suffix, q_width = queries.shape
    n_prefix = prefix.shape[0]
    n_rows = n_prefix + n_slot // 2 * tile + n_suffix
    n_prompt = lax.axis_size("prompt")
    vmem = pl.BlockSpec(memory_space=pltpu.VMEM)
    smem = pl.BlockSpec(memory_space=pltpu.SMEM)
    hbm = pl.BlockSpec(memory_space=pl.ANY)
    dma = pltpu.SemaphoreType.DMA
    return pl.pallas_call(
        judge_kernel,
        in_specs=[smem, smem, hbm, hbm, hbm, hbm, vmem],
        out_specs=[vmem, vmem],
        out_shape=[
            pltpu.VMEM((n_suffix, q_width), jnp.bfloat16),
            jax.ShapeDtypeStruct((1, 1), jnp.float32),
        ],
        scratch_shapes=[pltpu.VMEM((n_slot, tile, 2 * HD), jnp.bfloat16)] * (3 * KVH) + [
            pltpu.VMEM((2, n_slot // 4, 2, n_prefix, HD), jnp.bfloat16),
            pltpu.VMEM(suffix.shape, jnp.bfloat16),
            pltpu.VMEM(queries.shape, jnp.bfloat16),
            pltpu.VMEM((n_rows, HD), jnp.bfloat16),
            pltpu.VMEM((HD + 16, n_rows), jnp.bfloat16),
            pltpu.VMEM((n_rows, n_suffix), jnp.float32),
            pltpu.VMEM((n_rows, n_suffix), jnp.float32),
            pltpu.VMEM((8, HD), jnp.float32),
            pltpu.VMEM((8, 128), jnp.int32),
            pltpu.VMEM((n_slot, 8, 128), jnp.int32),
            pltpu.SMEM((n_slot, 8, 128), jnp.int32),
            pltpu.VMEM((8, 128), jnp.float32),
            pltpu.VMEM((n_slot, 8, 128), jnp.float32),
            pltpu.VMEM((8, 128), jnp.float32),
            pltpu.VMEM((n_prompt, 8, 128), jnp.float32),
            dma((4,)), dma((KVH,)), dma((KVH,)), dma((KVH,)),
            dma(()), dma(()), dma((4,)), dma((4,)), dma((2,)),
            dma(()), dma(()), dma(()), dma(()),
        ],
        compiler_params=pltpu.CompilerParams(
            collective_id=0, has_side_effects=True, vmem_limit_bytes=52 << 20
        ),
        name="judge",
    )(plen, routes, patch, prefix, queries, suffix, head)


def per_device(patch_kv, routes, prefix_kv, prefix_len, queries, suffix_kv, score_head):
    context, advantage = judge(
        prefix_len, routes, patch_kv[0], prefix_kv[0], queries[0, 0], suffix_kv[0, 0],
        score_head.reshape(HEADS, HD),
    )
    return (context[None, None], advantage)


def solution(mesh):
    placed = (
        P("prompt", "slot", None, None),
        P("prompt", "slot"),
        P("prompt", None, "slot"),
        P("prompt"),
        P("prompt", "slot", None, None),
        P("prompt", "slot", None, None),
        P(),
    )
    return jax.shard_map(
        per_device,
        mesh=mesh,
        in_specs=placed,
        out_specs=(P("prompt", "slot", None, None), P("prompt", "slot")),
        check_vma=False,
    )
```

```python
import math

import jax
import jax.numpy as jnp
from jax import lax
from jax.experimental import pallas as pl
from jax.experimental.pallas import tpu as pltpu
from jax.sharding import PartitionSpec as P

HEADS = 64
KVH = 8
HD = 128
GROUPS = HEADS // KVH
MESH = pl.DeviceIdType.MESH
OFFSETS = (
    (1, 0, 0), (3, 0, 0), (0, 1, 0), (2, 0, 0), (1, 1, 0),
    (3, 1, 0), (0, 1, 1), (2, 1, 0), (1, 0, 1), (3, 0, 1),
    (2, 0, 1), (1, 1, 1), (3, 1, 1), (2, 1, 1), (0, 0, 1),
)
NEG = -1e30


def judge_kernel(
    plen_ref, routes_ref, patch_ref, prefix_ref, queries_ref, suffix_ref, head_ref,
    context, advantage_ref,
    *scratch,
):
    image = scratch[:KVH]
    staged = scratch[KVH:2 * KVH]
    packed = scratch[2 * KVH:3 * KVH]
    (
        prefix, suffix, queries, keys, values, scores_a, scores_b, acc,
        live, routes, routes_s, scores_out, scores_in, squares_out, squares_in,
        local_sem, stage_sem, tile_send, tile_recv,
        route_send, route_recv, prefix_send, prefix_recv, relay_sem,
        score_send, score_recv, square_send, square_recv,
    ) = scratch[3 * KVH:]
    me = lax.axis_index("slot")
    prompt = lax.axis_index("prompt")
    n_slot = lax.axis_size("slot")
    n_prompt = lax.axis_size("prompt")
    x, y, c = me // 4, (me // 2) % 2, me % 2
    n_rows = keys.shape[0]
    n_prefix = prefix.shape[3]
    n_suffix = suffix.shape[0]
    tile = image[0].shape[1]
    n_tiles = (n_rows - n_prefix - n_suffix) // tile

    def peer(offset):
        tx = lax.rem(x + offset[0], 4)
        ty = lax.rem(y + offset[1], 2)
        tc = lax.rem(c + offset[2], 2)
        return (tx * 2 + ty) * 2 + tc

    def remote(src, dst, send, recv, **where):
        return pltpu.make_async_remote_copy(
            src, dst, send, recv, device_id=where, device_id_type=MESH
        )

    def stage(g):
        return [
            pltpu.make_async_copy(
                patch_ref.at[:, :, pl.ds(at * HD, HD)], staged[g].at[:, :, pl.ds(k * HD, HD)],
                stage_sem.at[g],
            )
            for k, at in enumerate((g, KVH + g))
        ]

    load_queries = pltpu.make_async_copy(queries_ref, queries, local_sem.at[0])
    load_suffix = pltpu.make_async_copy(suffix_ref, suffix, local_sem.at[1])
    load_prefix = pltpu.make_async_copy(prefix_ref, prefix.at[c, x, y], local_sem.at[2])
    for copy in stage(0) + stage(1):
        copy.start()
    load_prefix.start()
    barrier = pltpu.get_barrier_semaphore()
    for k in range(1, n_slot):
        pl.semaphore_signal(
            barrier, inc=1, device_id={"slot": lax.rem(me + k, n_slot)}, device_id_type=MESH
        )
    for k in range(1, n_prompt):
        pl.semaphore_signal(
            barrier, inc=1, device_id={"prompt": lax.rem(prompt + k, n_prompt)},
            device_id_type=MESH,
        )
    lane = lax.broadcasted_iota(jnp.int32, live.shape, 1)
    flags = jnp.zeros(live.shape, jnp.int32)
    slots = [jnp.int32(0)] * n_slot
    own_slot = jnp.int32(0)
    for k in range(n_slot):
        judge_of = routes_ref[0, k]
        flags = flags + jnp.where(lane == judge_of, 1, 0)
        own_slot = jnp.where(judge_of == me, jnp.int32(k), own_slot)
        for d in range(n_slot):
            slots[d] = jnp.where(judge_of == d, jnp.int32(k), slots[d])
    live[...] = flags
    routes[me] = flags
    def gather(g):
        for copy in stage(g):
            copy.wait()
        if g + 2 < KVH:
            for copy in stage(g + 2):
                copy.start()
        for d in range(n_slot):
            packed[g][d] = staged[g][slots[d]]
        image[g][me] = staged[g][own_slot]

    gather(0)
    gather(1)
    pl.semaphore_wait(barrier, n_slot + n_prompt - 2)

    cut = n_prefix * 13 // 32
    partner = peer((0, 1, 0))
    along = [peer((k, 0, 0)) for k in (1, 3, 2)]
    for target in along:
        remote(
            prefix_ref, prefix.at[c, x, y], prefix_send.at[0], prefix_recv.at[0], slot=target
        ).start()
    remote(
        prefix_ref.at[pl.ds(0, cut)], prefix.at[c, x, y, pl.ds(0, cut)],
        prefix_send.at[1], prefix_recv.at[1], slot=partner,
    ).start()
    for offset in OFFSETS:
        remote(live, routes.at[me], route_send, route_recv, slot=peer(offset)).start()
    whole = prefix.at[0, pl.ds(0, 3), 0]
    below = prefix.at[0, 0, 0, pl.ds(0, cut)]
    belows = prefix.at[0, pl.ds(0, 3), 0, pl.ds(0, cut)]
    rests = prefix.at[c, :, y, pl.ds(cut, n_prefix - cut)]

    def pass_prefix():
        load_prefix.wait()
        pltpu.make_async_copy(below, below, prefix_recv.at[1]).wait()
        theirs = prefix.at[c, x, 1 - y, pl.ds(0, cut)]
        for target in along:
            remote(
                theirs, theirs, prefix_send.at[2], prefix_recv.at[2], slot=target
            ).start()
        pltpu.make_async_copy(whole, whole, prefix_recv.at[0]).wait()
        remote(rests, rests, prefix_send.at[3], prefix_recv.at[3], slot=partner).start()

    def send_tiles(g):
        for offset in OFFSETS:
            target = peer(offset)
            remote(
                packed[g].at[target], image[g].at[me], tile_send.at[g], tile_recv.at[g],
                slot=target,
            ).start()

    send_tiles(0)
    send_tiles(1)
    pass_prefix()
    for g in range(2, KVH):
        gather(g)
        if g > 2:
            send_tiles(g - 1)
    send_tiles(KVH - 1)
    load_suffix.start()
    load_queries.start()

    pltpu.make_async_copy(belows, belows, prefix_recv.at[2]).wait()
    pltpu.make_async_copy(rests, rests, prefix_recv.at[3]).wait()
    relay = remote(
        prefix.at[c], prefix.at[c], relay_sem.at[0], relay_sem.at[1], slot=me + 1 - 2 * c
    )
    relay.start()

    arrived = routes.at[pl.ds(0, n_slot - 1)]
    pltpu.make_async_copy(arrived, arrived, route_recv).wait()
    fetch = pltpu.make_async_copy(routes, routes_s, local_sem.at[3])
    fetch.start()
    fetch.wait()
    index = [jnp.int32(0)] * n_tiles
    count = jnp.int32(0)
    for s in range(n_slot):
        alive = routes_s[s, 0, me]
        for j in range(n_tiles):
            index[j] = jnp.where(
                jnp.logical_and(alive > 0, count == j), jnp.int32(s), index[j]
            )
        count = count + jnp.where(alive > 0, 1, 0)

    inside = lax.broadcasted_iota(jnp.int32, (16, n_prefix), 1) < plen_ref[0]
    values[HD:, :n_prefix] = jnp.where(inside, 1.0, 0.0).astype(jnp.bfloat16)
    values[HD:, n_prefix:] = jnp.ones((16, n_rows - n_prefix), jnp.bfloat16)
    acc[...] = jnp.zeros_like(acc)
    load_suffix.wait()
    load_queries.wait()
    relay.wait()

    step = math.log2(math.e) / math.sqrt(HD)
    above = n_rows - n_suffix

    def add_score(rows, h):
        acc[...] += rows.astype(jnp.float32) * head_ref[pl.ds(h, 1), :]

    def score_last_rows(first):
        tail = jnp.concatenate(
            [
                queries[n_suffix - 16:, (first + i) * HD:(first + i + 1) * HD]
                for i in range(GROUPS)
            ],
            axis=0,
        )
        scores = lax.dot_general(
            keys[...], tail, (((1,), (1,)), ((), ())), preferred_element_type=jnp.float32
        )
        peak = jnp.max(scores, axis=0, keepdims=True)
        weights = jnp.exp2((scores - peak) * step).astype(jnp.bfloat16)
        mixed = jnp.dot(values[...], weights, preferred_element_type=jnp.float32)
        rounded = (mixed[:HD] / mixed[HD:HD + 1]).T.astype(jnp.bfloat16)
        for i in range(GROUPS):
            add_score(rounded[16 * i + 8:16 * i + 16, :], first + i)

    def score_head(scores, h):
        at = pl.multiple_of(h * HD, HD)
        query = queries[:, pl.ds(at, HD)]
        for rows in (pl.ds(0, n_rows // 2), pl.ds(n_rows // 2, n_rows // 2)):
            scores[rows, :] = lax.dot_general(
                keys[rows, :], query, (((1,), (1,)), ((), ())),
                preferred_element_type=jnp.float32,
            )

    def mix_head(scores, h, score):
        seen = scores[:above, :]
        own = scores[above:, :]
        keep = lax.broadcasted_iota(jnp.int32, own.shape, 0) <= lax.broadcasted_iota(
            jnp.int32, own.shape, 1
        )
        own = jnp.where(keep, own, NEG)
        peak = jnp.maximum(
            jnp.max(seen, axis=0, keepdims=True), jnp.max(own, axis=0, keepdims=True)
        )
        w_seen = jnp.exp2((seen - peak) * step).astype(jnp.bfloat16)
        w_own = jnp.exp2((own - peak) * step).astype(jnp.bfloat16)
        weights = jnp.concatenate([w_seen, w_own], axis=0)
        mixed = jnp.dot(values[...], weights, preferred_element_type=jnp.float32)
        rounded = (mixed[:HD] / mixed[HD:HD + 1]).T.astype(jnp.bfloat16)
        at = pl.multiple_of(h * HD, HD)
        context[:, pl.ds(at, HD)] = rounded
        if score:
            add_score(rounded[n_suffix - 8:, :], h)

    def build(g, pieces):
        k_prefix = prefix[lax.rem(g, 2), g // 4, lax.rem(g // 2, 2)].astype(jnp.float32)
        v_prefix = prefix[lax.rem(g, 2), 2 + g // 4, lax.rem(g // 2, 2)].astype(jnp.float32)
        inside = lax.broadcasted_iota(jnp.int32, (n_prefix, HD), 0) < plen_ref[0]
        keys[:n_prefix, :] = jnp.where(inside, k_prefix, k_prefix[0:1, :]).astype(jnp.bfloat16)
        values[:HD, :n_prefix] = jnp.where(inside, v_prefix, 0.0).T.astype(jnp.bfloat16)
        k_at = pl.multiple_of(g * HD, HD)
        v_at = pl.multiple_of((KVH + g) * HD, HD)
        keys[above:, :] = suffix[:, pl.ds(k_at, HD)]
        values[:HD, above:] = suffix[:, pl.ds(v_at, HD)].T
        for k in pieces:
            @pl.when(g == k)
            def _():
                landed = image[k].at[pl.ds(0, n_slot - 1)]
                pltpu.make_async_copy(landed, landed, tile_recv.at[k]).wait()
                for j in range(n_tiles):
                    at = n_prefix + j * tile
                    keys[at:at + tile, :] = image[k][index[j], :, :HD]
                    values[:HD, at:at + tile] = image[k][index[j], :, HD:].T


    def two_heads(first, i, score):
        last = first + GROUPS - 1
        h = first + 2 * i
        score_head(scores_b, h + 1)
        mix_head(scores_a, h, score)
        score_head(scores_a, jnp.minimum(h + 2, last))
        mix_head(scores_b, h + 1, score)

    def one_group(g, carry):
        build(g, range(KVH - 1))
        first = g * GROUPS
        score_head(scores_a, first)

        def body(i, carry):
            two_heads(first, i, True)
            return carry

        lax.fori_loop(0, GROUPS // 2, body, 0)
        return carry

    lax.fori_loop(0, KVH - 1, one_group, 0)

    final = KVH - 1
    build(final, [final])
    score_last_rows(final * GROUPS)
    score = jnp.sum(acc[7:8, :], axis=1, keepdims=True)
    score = jnp.broadcast_to(score, scores_out.shape)
    scores_out[...] = score
    for offset in OFFSETS:
        remote(scores_out, scores_in.at[me], score_send, score_recv, slot=peer(offset)).start()
    scores_in[me] = score
    score_head(scores_a, final * GROUPS)

    def early(i, carry):
        two_heads(final * GROUPS, i, False)
        return carry

    lax.fori_loop(0, GROUPS // 4, early, 0)
    arrived = scores_in.at[pl.ds(0, n_slot - 1)]
    pltpu.make_async_copy(arrived, arrived, score_recv).wait()
    centre = jnp.sum(scores_in[...], axis=0) / n_slot
    deviation = scores_in[...] - centre[None]
    squares = jnp.sum(deviation * deviation, axis=0)
    squares_out[...] = squares
    for k in range(1, n_prompt):
        remote(
            squares_out, squares_in.at[prompt], square_send, square_recv,
            prompt=lax.rem(prompt + k, n_prompt),
        ).start()
    squares_in[prompt] = squares
    lax.fori_loop(GROUPS // 4, GROUPS // 2, early, 0)
    arrived_p = squares_in.at[pl.ds(0, n_prompt - 1)]
    pltpu.make_async_copy(arrived_p, arrived_p, square_recv).wait()
    spread = jnp.sum(squares_in[...], axis=0) / (n_slot * n_prompt)
    result = (score - centre) / jnp.sqrt(spread + 1e-06)
    advantage_ref[...] = result[0:1, 0:1]

    pltpu.make_async_copy(arrived, arrived, score_send).wait()
    pltpu.make_async_copy(arrived_p, arrived_p, square_send).wait()
    sent = routes.at[pl.ds(0, n_slot - 1)]
    pltpu.make_async_copy(sent, sent, route_send).wait()
    for k, done in enumerate((whole, below, belows, rests)):
        pltpu.make_async_copy(done, done, prefix_send.at[k]).wait()
    for k in range(KVH):
        landed = image[k].at[pl.ds(0, n_slot - 1)]
        pltpu.make_async_copy(landed, landed, tile_send.at[k]).wait()


def judge(plen, routes, patch, prefix, queries, suffix, head):
    n_slot, tile, width = patch.shape
    n_suffix, q_width = queries.shape
    n_prefix = prefix.shape[0]
    n_rows = n_prefix + n_slot // 2 * tile + n_suffix
    n_prompt = lax.axis_size("prompt")
    vmem = pl.BlockSpec(memory_space=pltpu.VMEM)
    smem = pl.BlockSpec(memory_space=pltpu.SMEM)
    hbm = pl.BlockSpec(memory_space=pl.ANY)
    dma = pltpu.SemaphoreType.DMA
    return pl.pallas_call(
        judge_kernel,
        in_specs=[smem, smem, hbm, hbm, hbm, hbm, vmem],
        out_specs=[vmem, vmem],
        out_shape=[
            pltpu.VMEM((n_suffix, q_width), jnp.bfloat16),
            jax.ShapeDtypeStruct((1, 1), jnp.float32),
        ],
        scratch_shapes=[pltpu.VMEM((n_slot, tile, 2 * HD), jnp.bfloat16)] * (3 * KVH) + [
            pltpu.VMEM((2, n_slot // 4, 2, n_prefix, HD), jnp.bfloat16),
            pltpu.VMEM(suffix.shape, jnp.bfloat16),
            pltpu.VMEM(queries.shape, jnp.bfloat16),
            pltpu.VMEM((n_rows, HD), jnp.bfloat16),
            pltpu.VMEM((HD + 16, n_rows), jnp.bfloat16),
            pltpu.VMEM((n_rows, n_suffix), jnp.float32),
            pltpu.VMEM((n_rows, n_suffix), jnp.float32),
            pltpu.VMEM((8, HD), jnp.float32),
            pltpu.VMEM((8, 128), jnp.int32),
            pltpu.VMEM((n_slot, 8, 128), jnp.int32),
            pltpu.SMEM((n_slot, 8, 128), jnp.int32),
            pltpu.VMEM((8, 128), jnp.float32),
            pltpu.VMEM((n_slot, 8, 128), jnp.float32),
            pltpu.VMEM((8, 128), jnp.float32),
            pltpu.VMEM((n_prompt, 8, 128), jnp.float32),
            dma((4,)), dma((KVH,)), dma((KVH,)), dma((KVH,)),
            dma(()), dma(()), dma((4,)), dma((4,)), dma((2,)),
            dma(()), dma(()), dma(()), dma(()),
        ],
        compiler_params=pltpu.CompilerParams(
            collective_id=0, has_side_effects=True, vmem_limit_bytes=52 << 20
        ),
        name="judge",
    )(plen, routes, patch, prefix, queries, suffix, head)


def per_device(patch_kv, routes, prefix_kv, prefix_len, queries, suffix_kv, score_head):
    context, advantage = judge(
        prefix_len, routes, patch_kv[0], prefix_kv[0], queries[0, 0], suffix_kv[0, 0],
        score_head.reshape(HEADS, HD),
    )
    return (context[None, None], advantage)


def solution(mesh):
    placed = (
        P("prompt", "slot", None, None),
        P("prompt", "slot"),
        P("prompt", None, "slot"),
        P("prompt"),
        P("prompt", "slot", None, None),
        P("prompt", "slot", None, None),
        P(),
    )
    return jax.shard_map(
        per_device,
        mesh=mesh,
        in_specs=placed,
        out_specs=(P("prompt", "slot", None, None), P("prompt", "slot")),
        check_vma=False,
    )
```
